32 devices in a mesh: dp: 16 (over z, y, x), mp: 2 (over core).
Axes of the slice: x: 2, y: 2, z: 4, core: 2. Of those that a mesh axis runs over, the one named last changes fastest.
Arguments:
- tokens: bfloat16 [16, 1024, 1024], P('dp'), may hold values from -6 to 6
- doc_lengths: int32 [16, 8], P('dp'), may hold values from 1 to 384, 1024 in all within a row
- pad_counts: int32 [16], P('dp'), may hold values from 0 to 255
- norm_gain: float32 [4, 1024], replicated, may hold values from 0.5 to 1.5
- norm_bias: float32 [4, 1024], replicated, may hold values from -1.5 to 1.5
- qkv_weight: bfloat16 [1024, 3, 1024], P(None, None, 'mp'), may hold values from -0.1875 to 0.1875
- out_weight: bfloat16 [1024, 1024], P('mp'), may hold values from -0.1875 to 0.1875
- up_weight: bfloat16 [1024, 4096], P(None, 'mp'), may hold values from -0.1875 to 0.1875
- down_weight: bfloat16 [4096, 1024], P('mp'), may hold values from -0.09375 to 0.09375
- cotangent: bfloat16 [16, 1024, 1024], P('dp'), may hold values from -6 to 6
Outputs:
- out_tokens: bfloat16 [16, 1024, 1024], P('dp')
- input_grad: bfloat16 [16, 1024, 1024], P('dp')
- gain_grad: float32 [4, 1024], replicated
- bias_grad: float32 [4, 1024], replicated
- qkv_grad: float32 [1024, 3, 1024], P(None, None, 'mp')
- out_grad: float32 [1024, 1024], P('mp')
- up_grad: float32 [1024, 4096], P(None, 'mp')
- down_grad: float32 [4096, 1024], P('mp')
The draws below stay inside these ranges and needn't reach their ends.
Inputs may be any that keep to these rules, and one draw needn't show every extreme that they name: `doc_lengths`: the 8 document lengths of a row add up to 1024; the last pad_counts positions of a row are padding, whatever document they fall in.
All inputs are finite; a program needn't handle non-finite values.
Results may differ from the reference program's by a relative error of at most 0.02.
Values may be sent and summed in bfloat16 or wider, within the bound.
No kernel may reach another device: no remote copies, remote signals or barrier semaphores. Data moves between devices by JAX's collectives and lax.ppermute only.
A program may use at most 192 MiB of HBM per device.

```python
import math
import jax
import jax.numpy as jnp
import numpy as np
from jax import lax

D = 1024
HEADS = 16
HEAD_DIM = 64
FF = 4096
SEQ = 1024
NDOC = 8
DOC_MOST = 384
INNER = 1024
ROWS = 16
N_MP = 2


def place_ends(entries, own_key, least, largest):
    longest = entries.shape.index(max(entries.shape))
    spots = []
    for shift in (0, 1):
        where = [jax.random.randint(jax.random.fold_in(own_key, axis), (), 0, length) for axis, length in enumerate(entries.shape)]
        where[longest] = (where[longest] + shift) % entries.shape[longest]
        spots.append(tuple(where))
    return entries.at[spots[0]].set(least).at[spots[1]].set(largest)


def block_scale(rng, shape, pieces, low, top_value):
    level, own = 1.0, jax.random.fold_in(rng, 6)
    for dim, shards_of in pieces:
        steps = jnp.exp(jax.random.uniform(jax.random.fold_in(own, dim), (shards_of,), jnp.float32, low / len(pieces), top_value / len(pieces)))
        level = level * jnp.repeat(steps, shape[dim] // shards_of).reshape([-1 if axis == dim else 1 for axis in range(len(shape))])
    return level


def split_up(amount, total, bound, slope):
    weights = [(1 << 20) // math.isqrt(standing ** slope) + 1 for standing in range(2, amount + 1)]
    spare, holding = total - bound - (amount - 1), [1] * (amount - 1)
    while spare > 0:
        movable = [i for i in range(amount - 1) if holding[i] < bound]
        pool, budget = sum([weights[i] for i in movable]), spare
        for i in movable:
            addition = min(bound - holding[i], max(1, budget * weights[i] // pool), spare)
            holding[i] = holding[i] + addition
            spare = spare - addition
    return np.array([bound] + holding)


def ragged(key, count, total, limit, slope):
    if count == 2:
        one = jax.random.randint(key, (), max(1, total - limit), min(limit, total - 1) + 1)
        return jnp.stack([one, total - one])
    tallies = jnp.asarray(split_up(count, total, limit, slope), jnp.int32)
    pairs = (count - 1) // 2
    source_of, sink = tallies[1:1 + 2 * pairs:2], tallies[2:2 + 2 * pairs:2]
    room = jnp.minimum(source_of - 1, limit - sink)
    shifted = jax.random.randint(jax.random.fold_in(key, 1), (pairs,), 0, 1 << 20) % (room + 1)
    tallies = tallies.at[1:1 + 2 * pairs:2].set(source_of - shifted).at[2:2 + 2 * pairs:2].set(sink + shifted)
    return tallies[jax.random.permutation(jax.random.fold_in(key, 2), count)]


def normal_values(own_key, dims, width, reach, shards=(), kind=jnp.bfloat16):
    factor_of = block_scale(own_key, dims, shards, -0.22, 0.18) if shards else 1.0
    entries = jax.random.normal(own_key, dims, jnp.float32) * width * factor_of
    return jnp.minimum(jnp.maximum(entries, -reach), reach).astype(kind)


def setup_inputs(seed: int = 0) -> dict:
    key_list = jax.random.split(jax.random.key(seed), 11)
    tokens = normal_values(key_list[0], (ROWS, SEQ, D), 1.0, 6.0, ((0, 16),))
    doc_lengths = jax.vmap(lambda own: ragged(own, NDOC, SEQ, DOC_MOST, 2))(jax.random.split(key_list[1], ROWS)).reshape((ROWS, NDOC)).astype(jnp.int32)
    pad_counts = place_ends(jax.random.randint(key_list[2], (ROWS,), 0, SEQ // 4), jax.random.fold_in(key_list[2], 1), 0, (SEQ // 4) - 1).astype(jnp.int32)
    norm_gain = jnp.clip(1.0 + 0.1 * jax.random.normal(key_list[3], (4, D), jnp.float32), 0.5, 1.5)
    norm_bias = normal_values(key_list[4], (4, D), 0.3, 1.5, (), jnp.float32)
    qkv_weight = normal_values(key_list[5], (D, 3, INNER), D ** -0.5, 0.1875, ((2, 2),))
    out_weight = normal_values(key_list[6], (INNER, D), INNER ** -0.5, 0.1875, ((0, 2),))
    up_weight = normal_values(key_list[7], (D, FF), D ** -0.5, 0.1875, ((1, 2),))
    down_weight = normal_values(key_list[8], (FF, D), FF ** -0.5, 0.09375, ((0, 2),))
    cotangent = normal_values(key_list[9], (ROWS, SEQ, D), 1.0, 6.0, ((0, 16),))
    return {"tokens": tokens, "doc_lengths": doc_lengths, "pad_counts": pad_counts, "norm_gain": norm_gain, "norm_bias": norm_bias, "qkv_weight": qkv_weight, "out_weight": out_weight, "up_weight": up_weight, "down_weight": down_weight, "cotangent": cotangent}


EPSILON = 1e-05
NEGATIVE = -1e+30
GELU_SCALE = 0.7978845608028654
HIGHEST = lax.Precision.HIGHEST

@jax.custom_vjp
def low(v):
    return lax.optimization_barrier(v.astype(jnp.bfloat16)).astype(jnp.float32)

@jax.custom_vjp
def low_back(v):
    return v

def low_keep(v):
    return (low(v), None)

def low_pass(kept, grad):
    return (grad,)

def back_keep(v):
    return (v, None)

def back_low(kept, grad):
    return (low(grad),)
low.defvjp(low_keep, low_pass)
low_back.defvjp(back_keep, back_low)

def normalize(values_in, gain_vec, shift_vec):
    mean_vals = lax.optimization_barrier(jnp.mean(values_in, axis=-1, keepdims=True))
    centred = values_in - mean_vals
    spread = lax.optimization_barrier(jnp.mean(centred * centred, axis=-1, keepdims=True))
    return centred * lax.rsqrt(spread + EPSILON) * gain_vec + shift_vec

def gelu_tanh(hidden):
    return 0.5 * hidden * (1.0 + jnp.tanh(GELU_SCALE * (hidden + 0.044715 * hidden * hidden * hidden)))

def rotate(field_in, cosine, sine_vals):
    half_dim = field_in.shape[-1] // 2
    first_half = field_in[..., :half_dim]
    second_half = field_in[..., half_dim:]
    return jnp.concatenate([first_half * cosine - second_half * sine_vals, second_half * cosine + first_half * sine_vals], axis=-1)

def row_layout(lengths, pad_count, seq_len, half_dim):
    position = jnp.arange(seq_len, dtype=jnp.int32)
    doc_ends = jnp.cumsum(lengths).astype(jnp.int32)
    passed = position[:, None] >= doc_ends[None, :]
    segment = lax.optimization_barrier(jnp.sum(passed.astype(jnp.int32), axis=1)).astype(jnp.int32)
    start_at = lax.optimization_barrier(jnp.sum(jnp.where(passed, lengths[None, :], 0), axis=1)).astype(jnp.int32)
    pad_start = (seq_len - pad_count).astype(jnp.int32)
    is_live = position < pad_start
    segment = jnp.where(is_live, segment, lengths.shape[0]).astype(jnp.int32)
    start_at = jnp.where(is_live, start_at, pad_start).astype(jnp.int32)
    offset = (position - start_at).astype(jnp.float32)
    frequencies = jnp.exp(-math.log(10000.0) * jnp.arange(half_dim, dtype=jnp.float32) / half_dim)
    angles = offset[:, None] * frequencies[None, :]
    return (segment, position, jnp.cos(angles), jnp.sin(angles))

def layer_row(x_row, gain_all, shift_all, qkv_w, out_w, up_w, down_w, segment, position, cosine, sine_vals):
    normed = low(normalize(x_row, gain_all[0], shift_all[0]))
    mixed_proj = low_back(jnp.einsum('nd,dce->nce', normed, qkv_w, precision=HIGHEST))
    mixed_proj = mixed_proj.reshape(SEQ, 3, HEADS, HEAD_DIM)
    cos_heads = cosine[:, None, :]
    sin_heads = sine_vals[:, None, :]
    query_low = low(rotate(mixed_proj[:, 0], cos_heads, sin_heads))
    key_low = low(rotate(mixed_proj[:, 1], cos_heads, sin_heads))
    value_low = low(mixed_proj[:, 2])
    scores = jnp.einsum('qhd,khd->hqk', query_low, key_low, precision=HIGHEST) * HEAD_DIM ** (-0.5)
    scores = low_back(scores)
    allowed = (segment[:, None] == segment[None, :]) & (position[None, :] <= position[:, None])
    scores = jnp.where(allowed[None], scores, NEGATIVE)
    row_max = lax.optimization_barrier(jnp.max(scores, axis=-1, keepdims=True))
    expo_vals = jnp.exp(scores - row_max)
    soft_weights = low(expo_vals / lax.optimization_barrier(jnp.sum(expo_vals, axis=-1, keepdims=True)))
    attended = jnp.einsum('hqk,khd->qhd', soft_weights, value_low, precision=HIGHEST).reshape(SEQ, HEADS * HEAD_DIM)
    attended = low_back(low(attended))
    group_inner = HEADS * HEAD_DIM // N_MP
    att_parts = jnp.einsum('ngi,gid->gnd', attended.reshape(SEQ, N_MP, group_inner), out_w.reshape(N_MP, group_inner, D), precision=HIGHEST)
    att_sum = low_back(lax.optimization_barrier(jnp.sum(low(att_parts), axis=0)))
    middle_rows = x_row + normalize(att_sum, gain_all[1], shift_all[1])
    mlp_norm = low(normalize(middle_rows, gain_all[2], shift_all[2]))
    hidden = low_back(jnp.dot(mlp_norm, up_w, precision=HIGHEST))
    activated = low(gelu_tanh(hidden))
    group_hidden = FF // N_MP
    mlp_parts = jnp.einsum('ngi,gid->gnd', activated.reshape(SEQ, N_MP, group_hidden), down_w.reshape(N_MP, group_hidden, D), precision=HIGHEST)
    mlp_sum = low_back(lax.optimization_barrier(jnp.sum(low(mlp_parts), axis=0)))
    return middle_rows + normalize(mlp_sum, gain_all[3], shift_all[3])

def reference(tokens, doc_lengths, pad_counts, norm_gain, norm_bias, qkv_weight, out_weight, up_weight, down_weight, cotangent):
    params = (norm_gain.astype(jnp.float32), norm_bias.astype(jnp.float32), qkv_weight.astype(jnp.float32), out_weight.astype(jnp.float32), up_weight.astype(jnp.float32), down_weight.astype(jnp.float32))

    def row_step(carried, row_data):
        x_row, lengths, pad_count, grad_row = row_data
        segment, position, cosine, sine_vals = row_layout(lengths, pad_count, SEQ, HEAD_DIM // 2)

        def forward(x_in, weights):
            return layer_row(x_in, weights[0], weights[1], weights[2], weights[3], weights[4], weights[5], segment, position, cosine, sine_vals)
        output, backward = jax.vjp(forward, x_row.astype(jnp.float32), params)
        grad_x, grad_params = backward(grad_row.astype(jnp.float32))
        carried = jax.tree.map(jnp.add, carried, grad_params)
        return (carried, (output.astype(jnp.bfloat16), grad_x.astype(jnp.bfloat16)))
    zero_grads = jax.tree.map(jnp.zeros_like, params)
    grad_sums, (out_tokens, input_grad) = lax.scan(row_step, zero_grads, (tokens, doc_lengths, pad_counts, cotangent))
    return (out_tokens, input_grad, grad_sums[0], grad_sums[1], grad_sums[2], grad_sums[3], grad_sums[4], grad_sums[5])
```

```python
import functools
import math

import jax, jax.numpy as jnp
from jax import lax
from jax.experimental import pallas as pl
from jax.experimental.pallas import tpu as pltpu
from jax.sharding import PartitionSpec as P

HEAD_DIM = 64
DOC_MOST = 384
NEGATIVE = -1e30
BLOCK = 256
AUG = 16


def spans(seq_len):
    block = min(BLOCK, seq_len)
    return [(q, block, max(0, q - DOC_MOST)) for q in range(0, seq_len, block)]


def dot(a, b):
    return lax.dot_general(a, b, (((1,), (0,)), ((), ())), preferred_element_type=jnp.float32)


def spin(u, cosine, sine, sign):
    half = u.shape[0] // 2
    first, second = u[:half].astype(jnp.float32), u[half:].astype(jnp.float32)
    return first * cosine - sign * second * sine, second * cosine + sign * first * sine


def turned(ref, cosine, sine, scale):
    first, second = spin(ref[0], cosine, sine, 1.0)
    return jnp.concatenate([first * scale, second * scale], axis=0).astype(jnp.bfloat16)


def causal(block):
    key = lax.broadcasted_iota(jnp.int32, (block, block), 0)
    query = lax.broadcasted_iota(jnp.int32, (block, block), 1)
    return key <= query


def masked(scores, keep, block):
    last = jnp.where(keep, scores[-block:], NEGATIVE)
    if scores.shape[0] == block:
        return last
    return jnp.concatenate([scores[:-block], last], axis=0)


def setup(q_ref, k_ref, cos_ref, sin_ref, qaug_ref, kaug_ref, qt_scr, kn_scr):
    cosine, sine = cos_ref[...], sin_ref[...]
    seq_len = q_ref.shape[-1]
    pad = jnp.zeros((128 - HEAD_DIM - AUG, seq_len), jnp.bfloat16)
    q_low = turned(q_ref, cosine, sine, HEAD_DIM ** -0.5)
    k_low = turned(k_ref, cosine, sine, 1.0)
    qt_scr[...] = jnp.concatenate([q_low, qaug_ref[...], pad], axis=0)
    k_all = jnp.concatenate([k_low, kaug_ref[...], pad], axis=0)
    kn_scr[...] = k_all.T
    return q_low, k_low


def fwd_kernel(q_ref, k_ref, v_ref, cos_ref, sin_ref, qaug_ref, kaug_ref, o_ref, lse_ref, qt_scr, kn_scr):
    seq_len = q_ref.shape[-1]
    setup(q_ref, k_ref, cos_ref, sin_ref, qaug_ref, kaug_ref, qt_scr, kn_scr)
    for start, block, low in spans(seq_len):
        high = start + block
        scores = dot(kn_scr[low:high, :], qt_scr[:, start:high])
        scores = masked(scores, causal(block), block)
        top = jnp.max(scores, axis=0, keepdims=True)
        expo = jnp.exp(scores - top)
        total = jnp.sum(expo, axis=0, keepdims=True)
        out = dot(v_ref[0, :, low:high], expo.astype(jnp.bfloat16)) / total
        o_ref[:, start:high] = out.astype(jnp.bfloat16)
        lse_ref[0, :, start:high] = top + jnp.log(total)


def bwd_kernel(q_ref, k_ref, v_ref, cos_ref, sin_ref, qaug_ref, kaug_ref, o_ref, lse_ref, do_ref,
               dm_ref, qt_scr, kn_scr, qn_scr, kt_scr, vn_scr, don_scr, dk_scr, dv_scr):
    seq_len = q_ref.shape[-1]
    cosine, sine = cos_ref[...], sin_ref[...]
    q_low, k_low = setup(q_ref, k_ref, cos_ref, sin_ref, qaug_ref, kaug_ref, qt_scr, kn_scr)
    kt_scr[...] = k_low
    both = jnp.concatenate([q_low, do_ref[...]], axis=0).T
    qn_scr[...] = both[:, :HEAD_DIM]
    don_scr[...] = both[:, HEAD_DIM:]
    vn_scr[...] = v_ref[0].T
    dk_scr[...] = jnp.zeros_like(dk_scr)
    dv_scr[...] = jnp.zeros_like(dv_scr)
    inner = jnp.sum(o_ref[...].astype(jnp.float32) * do_ref[...].astype(jnp.float32), axis=0, keepdims=True)
    for start, block, low in spans(seq_len):
        high = start + block
        scores = dot(kn_scr[low:high, :], qt_scr[:, start:high])
        scores = masked(scores, causal(block), block)
        soft = jnp.exp(scores - lse_ref[0, :, start:high])
        d_soft = dot(vn_scr[low:high, :], do_ref[:, start:high])
        d_scores = (soft * (d_soft - inner[:, start:high])).astype(jnp.bfloat16)
        d_q = dot(kt_scr[:, low:high], d_scores) * HEAD_DIM ** -0.5
        first, second = spin(d_q, cosine[:, start:high], sine[:, start:high], -1.0)
        half = HEAD_DIM // 2
        dm_ref[0, :half, start:high] = first.astype(jnp.bfloat16)
        dm_ref[0, half:, start:high] = second.astype(jnp.bfloat16)
        dk_scr[low:high, :] += dot(d_scores, qn_scr[start:high, :])
        dv_scr[low:high, :] += dot(soft.astype(jnp.bfloat16), don_scr[start:high, :])
    first, second = spin(dk_scr[...].T, cosine, sine, -1.0)
    dm_ref[1] = jnp.concatenate([first, second], axis=0).astype(jnp.bfloat16)
    dm_ref[2] = dv_scr[...].T.astype(jnp.bfloat16)


def common_specs(seq_len):
    part = lambda c: pl.BlockSpec((1, HEAD_DIM, seq_len), lambda h: (c, h, 0))
    whole = lambda rows: pl.BlockSpec((rows, seq_len), lambda h: (0, 0))
    half = HEAD_DIM // 2
    return [part(0), part(1), part(2), whole(half), whole(half), whole(AUG), whole(AUG)]


def attention_forward(mixed, cosine, sine, qaug, kaug):
    _, inner, seq_len = mixed.shape
    heads = inner // HEAD_DIM
    head_spec = pl.BlockSpec((HEAD_DIM, seq_len), lambda h: (h, 0))
    return pl.pallas_call(
        fwd_kernel,
        grid=(heads,),
        in_specs=common_specs(seq_len),
        out_specs=[head_spec, pl.BlockSpec((1, 1, seq_len), lambda h: (h, 0, 0))],
        out_shape=[jax.ShapeDtypeStruct((inner, seq_len), jnp.bfloat16),
                   jax.ShapeDtypeStruct((heads, 1, seq_len), jnp.float32)],
        scratch_shapes=[pltpu.VMEM((128, seq_len), jnp.bfloat16), pltpu.VMEM((seq_len, 128), jnp.bfloat16)],
        name="attention_forward",
        cost_estimate=pl.CostEstimate(flops=heads * 2 * 2 * seq_len * 512 * 128, bytes_accessed=inner * seq_len * 8, transcendentals=heads * seq_len * 512),
    )(mixed, mixed, mixed, cosine, sine, qaug, kaug)


def attention_backward(mixed, cosine, sine, qaug, kaug, att, lse, d_att):
    _, inner, seq_len = mixed.shape
    heads = inner // HEAD_DIM
    head_spec = pl.BlockSpec((HEAD_DIM, seq_len), lambda h: (h, 0))
    return pl.pallas_call(
        bwd_kernel,
        grid=(heads,),
        in_specs=common_specs(seq_len) + [head_spec, pl.BlockSpec((1, 1, seq_len), lambda h: (h, 0, 0)), head_spec],
        out_specs=pl.BlockSpec((3, HEAD_DIM, seq_len), lambda h: (0, h, 0)),
        out_shape=jax.ShapeDtypeStruct(mixed.shape, jnp.bfloat16),
        scratch_shapes=[pltpu.VMEM((128, seq_len), jnp.bfloat16), pltpu.VMEM((seq_len, 128), jnp.bfloat16),
                        pltpu.VMEM((seq_len, HEAD_DIM), jnp.bfloat16), pltpu.VMEM((HEAD_DIM, seq_len), jnp.bfloat16),
                        pltpu.VMEM((seq_len, HEAD_DIM), jnp.bfloat16), pltpu.VMEM((seq_len, HEAD_DIM), jnp.bfloat16),
                        pltpu.VMEM((seq_len, HEAD_DIM), jnp.float32), pltpu.VMEM((seq_len, HEAD_DIM), jnp.float32)],
        name="attention_backward",
        cost_estimate=pl.CostEstimate(flops=heads * 5 * 2 * seq_len * 512 * 128, bytes_accessed=inner * seq_len * 16, transcendentals=heads * seq_len * 512),
    )(mixed, mixed, mixed, cosine, sine, qaug, kaug, att, lse, d_att)


EPSILON = 1e-05
GELU_SCALE = 0.7978845608028654
SEGMENTS = 9
GRIDS = {16: (4, 2, 2)}


def normalize(values_in, gain_vec, shift_vec):
    mean_vals = jnp.mean(values_in, axis=-1, keepdims=True)
    centred = values_in - mean_vals
    spread = jnp.mean(centred * centred, axis=-1, keepdims=True)
    return centred * lax.rsqrt(spread + EPSILON) * gain_vec + shift_vec


def gelu_tanh(hidden):
    return (
        0.5 * hidden * (1.0 + jnp.tanh(GELU_SCALE * (hidden + 0.044715 * hidden * hidden * hidden)))
    )


def row_layout(lengths, pad_count, seq_len, half_dim):
    position = jnp.arange(seq_len, dtype=jnp.int32)
    doc_ends = jnp.cumsum(lengths)
    passed = position[None, :] >= doc_ends[:, None]
    segment = jnp.sum(passed.astype(jnp.int32), axis=0)
    start_at = jnp.sum(jnp.where(passed, lengths[:, None], 0), axis=0)
    pad_start = seq_len - pad_count
    is_live = position < pad_start
    segment = jnp.where(is_live, segment, lengths.shape[0])
    start_at = jnp.where(is_live, start_at, pad_start)
    offset = (position - start_at).astype(jnp.float32)
    frequencies = jnp.exp(-math.log(10000.0) * jnp.arange(half_dim, dtype=jnp.float32) / half_dim)
    angles = frequencies[:, None] * offset[None, :]
    kind = jnp.arange(AUG, dtype=jnp.int32)[:, None]
    same = kind == segment[None, :]
    query_mark = same.astype(jnp.bfloat16)
    key_mark = jnp.where(same | (kind >= SEGMENTS), 0.0, NEGATIVE).astype(jnp.bfloat16)
    return (jnp.cos(angles), jnp.sin(angles), query_mark, key_mark)


def first_norm(rows_in, gain_all, shift_all):
    return normalize(rows_in, gain_all[0], shift_all[0])


def middle(att_rows, resid_rows, gain_all, shift_all):
    middle_rows = resid_rows + normalize(att_rows, gain_all[1], shift_all[1])
    return (middle_rows, normalize(middle_rows, gain_all[2], shift_all[2]))


def finish(mlp_rows, middle_rows, gain_all, shift_all):
    return middle_rows + normalize(mlp_rows, gain_all[3], shift_all[3])


def contract(left_side, right_side, left_dim, right_dim):
    return lax.dot_general(
        left_side, right_side, (((left_dim,), (right_dim,)), ((), ())), preferred_element_type=jnp.float32
    )


def low_add(one, other):
    return (one.astype(jnp.float32) + other.astype(jnp.float32)).astype(jnp.bfloat16)


class Grid:
    def __init__(self, sizes):
        self.sizes = sizes
        count = math.prod(sizes)
        x_size, y_size = sizes[2], sizes[1]
        plane = x_size * y_size
        self.x_pairs = [(i, i ^ 1) for i in range(count)]
        self.y_pairs = [(i, i ^ x_size) for i in range(count)]
        layer = lambda i: i // plane
        self.inward = [(i, i + plane) for i in range(count) if layer(i) == 0]
        self.inward += [(i, i - plane) for i in range(count) if layer(i) == 3]
        self.across = [(i, i + plane) for i in range(count) if layer(i) == 1]
        self.across += [(i, i - plane) for i in range(count) if layer(i) == 2]
        self.outward = [(b, a) for a, b in self.inward]
        index = lax.axis_index("dp")
        self.x_bit = index % x_size
        self.y_bit = (index // x_size) % y_size
        place = index // plane
        self.at_end = (place == 0) | (place == 3)

    def swap(self, values, pairs):
        return lax.ppermute(values, "dp", pairs)

    def line(self, values):
        values = low_add(values, self.swap(values, self.inward))
        values = low_add(values, self.swap(values, self.across))
        return jnp.where(self.at_end, self.swap(values, self.outward), values)

    def small(self, values):
        values = low_add(values, self.swap(values, self.x_pairs))
        values = low_add(values, self.swap(values, self.y_pairs))
        return self.line(values)

    def colour(self, values, x_first):
        order = [(self.x_pairs, self.x_bit), (self.y_pairs, self.y_bit)]
        if not x_first:
            order = order[::-1]
        for pairs, bit in order:
            half = values.shape[0] // 2
            send = lax.dynamic_slice_in_dim(values, (1 - bit) * half, half, 0)
            keep = lax.dynamic_slice_in_dim(values, bit * half, half, 0)
            values = low_add(keep, self.swap(send, pairs))
        values = self.line(values)
        pairs, bit = order[1]
        other = self.swap(values, pairs)
        quarter = values.shape[0]
        joined = jnp.concatenate([jnp.where(bit == 0, values, other), jnp.where(bit == 0, other, values)], axis=0)
        pairs, bit = order[0]
        return joined, self.swap(joined, pairs), bit

    def large(self, values, parts):
        half = values.shape[0] // 2
        pieces = []
        bits = []
        for colour in range(2):
            own, other, bit = self.colour(values[colour * half:(colour + 1) * half], colour == 0)
            pieces += [own, other]
            bits.append(bit)
        return assemble(jnp.stack(bits).astype(jnp.int32), pieces, parts)


def assemble_kernel(parts, bits_ref, own_a, other_a, own_b, other_b, out_ref):
    for colour, own, other in ((0, own_a, other_a), (1, own_b, other_b)):
        bit = bits_ref[colour]
        for slot, piece in ((2 * colour + bit, own), (2 * colour + 1 - bit, other)):
            if parts == 1:
                out_ref[slot] = piece[...].astype(jnp.float32)
            else:
                width = piece.shape[1] // parts
                for part in range(parts):
                    out_ref[slot, :, part, :] = piece[:, part * width:(part + 1) * width].astype(jnp.float32)


def assemble(bits, pieces, parts):
    rows, width = pieces[0].shape
    block = 32
    in_spec = pl.BlockSpec((block, width), lambda i, b: (i, 0))
    if parts == 1:
        shape, out_block, out_map = (4, rows, width), (4, block, width), lambda i, b: (0, i, 0)
    else:
        shape, out_block, out_map = (4, rows, parts, width // parts), (4, block, parts, width // parts), lambda i, b: (0, i, 0, 0)
    out = pl.pallas_call(
        functools.partial(assemble_kernel, parts),
        grid_spec=pltpu.PrefetchScalarGridSpec(
            num_scalar_prefetch=1,
            grid=(rows // block,),
            in_specs=[in_spec] * 4,
            out_specs=pl.BlockSpec(out_block, out_map),
        ),
        out_shape=jax.ShapeDtypeStruct(shape, jnp.float32),
        name="assemble",
        cost_estimate=pl.CostEstimate(flops=0, bytes_accessed=4 * rows * width * 6, transcendentals=0),
    )(bits, *pieces)
    return out.reshape((4 * rows,) + shape[2:])


def make_body(sizes):
    mp_size = sizes["mp"]
    grid_sizes = GRIDS.get(sizes["dp"])

    def pair_sum(partial_sum):
        low_part = partial_sum.astype(jnp.bfloat16)
        if mp_size == 2:
            other = lax.ppermute(low_part, "mp", [(0, 1), (1, 0)])
            return low_part.astype(jnp.float32) + other.astype(jnp.float32)
        return lax.psum(low_part, "mp").astype(jnp.float32)

    def plain_sum(values):
        return lax.psum(values.astype(jnp.bfloat16), "dp").astype(jnp.float32)

    def body(tokens, doc_lengths, pad_counts, norm_gain, norm_bias, qkv_weight, out_weight, up_weight, down_weight, cotangent):
        row_count, seq_len, width_all = tokens.shape
        token_count = row_count * seq_len
        inner_here = qkv_weight.shape[2]
        layouts = [row_layout(doc_lengths[r], pad_counts[r], seq_len, HEAD_DIM // 2) for r in range(row_count)]

        residual = tokens.reshape(token_count, width_all).astype(jnp.float32)
        normed_low = first_norm(residual, norm_gain, norm_bias).astype(jnp.bfloat16)
        mixed = contract(qkv_weight, normed_low, 0, 1).astype(jnp.bfloat16)
        spans_of = [slice(r * seq_len, (r + 1) * seq_len) for r in range(row_count)]
        forward = [attention_forward(mixed[:, :, s], *layout) for s, layout in zip(spans_of, layouts)]
        att_turned = jnp.concatenate([f[0] for f in forward], axis=1)
        att_sum = pair_sum(contract(att_turned, out_weight, 0, 0))
        middle_rows, mlp_norm = middle(att_sum, residual, norm_gain, norm_bias)
        mlp_low = mlp_norm.astype(jnp.bfloat16)
        hidden = contract(mlp_low, up_weight, 1, 0)
        act_low = gelu_tanh(hidden).astype(jnp.bfloat16)
        mlp_sum = pair_sum(contract(act_low, down_weight, 1, 0))
        output_rows = finish(mlp_sum, middle_rows, norm_gain, norm_bias)
        out_tokens = output_rows.astype(jnp.bfloat16).reshape(row_count, seq_len, width_all)
        grad_out = cotangent.reshape(token_count, width_all).astype(jnp.float32)
        _, finish_back = jax.vjp(finish, mlp_sum, middle_rows, norm_gain, norm_bias)
        grad_mlp_sum, grad_middle, gain_last, bias_last = finish_back(grad_out)
        grad_mlp_low = grad_mlp_sum.astype(jnp.bfloat16)
        down_grad = contract(act_low, grad_mlp_low, 0, 0).astype(jnp.bfloat16)
        down_sum = plain_sum(down_grad)
        grad_act = contract(grad_mlp_low, down_weight, 1, 1)
        _, gelu_back = jax.vjp(gelu_tanh, hidden)
        grad_hidden = gelu_back(grad_act)[0].astype(jnp.bfloat16)
        up_grad = contract(mlp_low, grad_hidden, 0, 0).astype(jnp.bfloat16)
        grad_mlp_norm = pair_sum(contract(grad_hidden, up_weight, 1, 1))
        _, middle_back = jax.vjp(middle, att_sum, residual, norm_gain, norm_bias)
        grad_att_sum, grad_resid_mid, gain_mid, bias_mid = middle_back((grad_middle, grad_mlp_norm))
        grad_att_low = grad_att_sum.astype(jnp.bfloat16)
        out_grad = contract(att_turned, grad_att_low, 1, 0).astype(jnp.bfloat16)
        grad_attended = contract(out_weight, grad_att_low, 1, 1).astype(jnp.bfloat16)
        grad_mixed = [
            attention_backward(mixed[:, :, s], *layout, f[0], f[1], grad_attended[:, s])
            for s, layout, f in zip(spans_of, layouts, forward)
        ]
        grad_mixed = jnp.concatenate(grad_mixed, axis=2)
        flat_mixed = grad_mixed.reshape(3 * inner_here, token_count)
        qkv_grad = contract(normed_low, flat_mixed, 0, 1).astype(jnp.bfloat16)
        grad_normed = pair_sum(
            lax.dot_general(
                grad_mixed, qkv_weight, (((0, 1), (1, 2)), ((), ())), preferred_element_type=jnp.float32
            )
        )
        _, first_back = jax.vjp(first_norm, residual, norm_gain, norm_bias)
        grad_resid_first, gain_first, bias_first = first_back(grad_normed)
        input_grad = (
            (grad_resid_mid + grad_resid_first)
            .astype(jnp.bfloat16)
            .reshape(row_count, seq_len, width_all)
        )
        small = jnp.concatenate([gain_last + gain_mid + gain_first, bias_last + bias_mid + bias_first], axis=0)
        if grid_sizes is None:
            qkv_sum = plain_sum(qkv_grad).reshape(width_all, 3, inner_here)
            out_sum, up_sum, small_sum = plain_sum(out_grad), plain_sum(up_grad), plain_sum(small)
        else:
            grid = Grid(grid_sizes)
            up_sum = grid.large(up_grad, 1)
            out_sum = grid.small(out_grad).astype(jnp.float32)
            qkv_sum = grid.large(qkv_grad, 3)
            small_sum = grid.small(small.astype(jnp.bfloat16)).astype(jnp.float32)
        norms = norm_gain.shape[0]
        return (out_tokens, input_grad, small_sum[:norms], small_sum[norms:], qkv_sum, out_sum, up_sum, down_sum)

    return body


def solution(mesh):
    in_specs = (
        P("dp", None, None),
        P("dp", None),
        P("dp"),
        P(),
        P(),
        P(None, None, "mp"),
        P("mp", None),
        P(None, "mp"),
        P("mp", None),
        P("dp", None, None),
    )
    out_specs = (
        P("dp", None, None),
        P("dp", None, None),
        P(),
        P(),
        P(None, None, "mp"),
        P("mp", None),
        P(None, "mp"),
        P("mp", None),
    )
    return jax.shard_map(make_body(dict(mesh.shape)), mesh=mesh, in_specs=in_specs, out_specs=out_specs, check_vma=False)
```

```python
import functools
import math

import jax, jax.numpy as jnp
from jax import lax
from jax.experimental import pallas as pl
from jax.experimental.pallas import tpu as pltpu
from jax.sharding import PartitionSpec as P

HEAD_DIM = 64
DOC_MOST = 384
NEGATIVE = -1e30
BLOCK = 256
AUG = 16


def spans(seq_len):
    block = min(BLOCK, seq_len)
    return [(q, block, max(0, q - DOC_MOST)) for q in range(0, seq_len, block)]


def dot(a, b):
    return lax.dot_general(a, b, (((1,), (0,)), ((), ())), preferred_element_type=jnp.float32)


def spin(u, cosine, sine, sign):
    half = u.shape[0] // 2
    first, second = u[:half].astype(jnp.float32), u[half:].astype(jnp.float32)
    return first * cosine - sign * second * sine, second * cosine + sign * first * sine


def turned(ref, cosine, sine, scale):
    first, second = spin(ref[0], cosine, sine, 1.0)
    return jnp.concatenate([first * scale, second * scale], axis=0).astype(jnp.bfloat16)


def causal(block):
    key = lax.broadcasted_iota(jnp.int32, (block, block), 0)
    query = lax.broadcasted_iota(jnp.int32, (block, block), 1)
    return key <= query


def masked(scores, keep, block):
    last = jnp.where(keep, scores[-block:], NEGATIVE)
    if scores.shape[0] == block:
        return last
    return jnp.concatenate([scores[:-block], last], axis=0)


def setup(q_ref, k_ref, cos_ref, sin_ref, qaug_ref, kaug_ref, qt_scr, kn_scr):
    cosine, sine = cos_ref[...], sin_ref[...]
    seq_len = q_ref.shape[-1]
    pad = jnp.zeros((128 - HEAD_DIM - AUG, seq_len), jnp.bfloat16)
    q_low = turned(q_ref, cosine, sine, HEAD_DIM ** -0.5)
    k_low = turned(k_ref, cosine, sine, 1.0)
    qt_scr[...] = jnp.concatenate([q_low, qaug_ref[...], pad], axis=0)
    k_all = jnp.concatenate([k_low, kaug_ref[...], pad], axis=0)
    kn_scr[...] = k_all.T
    return q_low, k_low


def fwd_kernel(q_ref, k_ref, v_ref, cos_ref, sin_ref, qaug_ref, kaug_ref, o_ref, lse_ref, qt_scr, kn_scr):
    seq_len = q_ref.shape[-1]
    setup(q_ref, k_ref, cos_ref, sin_ref, qaug_ref, kaug_ref, qt_scr, kn_scr)
    for start, block, low in spans(seq_len):
        high = start + block
        scores = dot(kn_scr[low:high, :], qt_scr[:, start:high])
        scores = masked(scores, causal(block), block)
        top = jnp.max(scores, axis=0, keepdims=True)
        expo = jnp.exp(scores - top)
        total = jnp.sum(expo, axis=0, keepdims=True)
        out = dot(v_ref[0, :, low:high], expo.astype(jnp.bfloat16)) / total
        o_ref[:, start:high] = out.astype(jnp.bfloat16)
        lse_ref[0, :, start:high] = top + jnp.log(total)


def bwd_kernel(q_ref, k_ref, v_ref, cos_ref, sin_ref, qaug_ref, kaug_ref, o_ref, lse_ref, do_ref,
               dm_ref, qt_scr, kn_scr, qn_scr, kt_scr, vn_scr, don_scr, dk_scr, dv_scr):
    seq_len = q_ref.shape[-1]
    cosine, sine = cos_ref[...], sin_ref[...]
    q_low, k_low = setup(q_ref, k_ref, cos_ref, sin_ref, qaug_ref, kaug_ref, qt_scr, kn_scr)
    kt_scr[...] = k_low
    both = jnp.concatenate([q_low, do_ref[...]], axis=0).T
    qn_scr[...] = both[:, :HEAD_DIM]
    don_scr[...] = both[:, HEAD_DIM:]
    vn_scr[...] = v_ref[0].T
    dk_scr[...] = jnp.zeros_like(dk_scr)
    dv_scr[...] = jnp.zeros_like(dv_scr)
    inner = jnp.sum(o_ref[...].astype(jnp.float32) * do_ref[...].astype(jnp.float32), axis=0, keepdims=True)
    for start, block, low in spans(seq_len):
        high = start + block
        scores = dot(kn_scr[low:high, :], qt_scr[:, start:high])
        scores = masked(scores, causal(block), block)
        soft = jnp.exp(scores - lse_ref[0, :, start:high])
        d_soft = dot(vn_scr[low:high, :], do_ref[:, start:high])
        d_scores = (soft * (d_soft - inner[:, start:high])).astype(jnp.bfloat16)
        d_q = dot(kt_scr[:, low:high], d_scores) * HEAD_DIM ** -0.5
        first, second = spin(d_q, cosine[:, start:high], sine[:, start:high], -1.0)
        half = HEAD_DIM // 2
        dm_ref[0, :half, start:high] = first.astype(jnp.bfloat16)
        dm_ref[0, half:, start:high] = second.astype(jnp.bfloat16)
        dk_scr[low:high, :] += dot(d_scores, qn_scr[start:high, :])
        dv_scr[low:high, :] += dot(soft.astype(jnp.bfloat16), don_scr[start:high, :])
    first, second = spin(dk_scr[...].T, cosine, sine, -1.0)
    dm_ref[1] = jnp.concatenate([first, second], axis=0).astype(jnp.bfloat16)
    dm_ref[2] = dv_scr[...].T.astype(jnp.bfloat16)


def common_specs(seq_len):
    part = lambda c: pl.BlockSpec((1, HEAD_DIM, seq_len), lambda h: (c, h, 0))
    whole = lambda rows: pl.BlockSpec((rows, seq_len), lambda h: (0, 0))
    half = HEAD_DIM // 2
    return [part(0), part(1), part(2), whole(half), whole(half), whole(AUG), whole(AUG)]


def attention_forward(mixed, cosine, sine, qaug, kaug):
    _, inner, seq_len = mixed.shape
    heads = inner // HEAD_DIM
    head_spec = pl.BlockSpec((HEAD_DIM, seq_len), lambda h: (h, 0))
    return pl.pallas_call(
        fwd_kernel,
        grid=(heads,),
        in_specs=common_specs(seq_len),
        out_specs=[head_spec, pl.BlockSpec((1, 1, seq_len), lambda h: (h, 0, 0))],
        out_shape=[jax.ShapeDtypeStruct((inner, seq_len), jnp.bfloat16),
                   jax.ShapeDtypeStruct((heads, 1, seq_len), jnp.float32)],
        scratch_shapes=[pltpu.VMEM((128, seq_len), jnp.bfloat16), pltpu.VMEM((seq_len, 128), jnp.bfloat16)],
        name="attention_forward",
        cost_estimate=pl.CostEstimate(flops=heads * 2 * 2 * seq_len * 512 * 128, bytes_accessed=inner * seq_len * 8, transcendentals=heads * seq_len * 512),
    )(mixed, mixed, mixed, cosine, sine, qaug, kaug)


def attention_backward(mixed, cosine, sine, qaug, kaug, att, lse, d_att):
    _, inner, seq_len = mixed.shape
    heads = inner // HEAD_DIM
    head_spec = pl.BlockSpec((HEAD_DIM, seq_len), lambda h: (h, 0))
    return pl.pallas_call(
        bwd_kernel,
        grid=(heads,),
        in_specs=common_specs(seq_len) + [head_spec, pl.BlockSpec((1, 1, seq_len), lambda h: (h, 0, 0)), head_spec],
        out_specs=pl.BlockSpec((3, HEAD_DIM, seq_len), lambda h: (0, h, 0)),
        out_shape=jax.ShapeDtypeStruct(mixed.shape, jnp.bfloat16),
        scratch_shapes=[pltpu.VMEM((128, seq_len), jnp.bfloat16), pltpu.VMEM((seq_len, 128), jnp.bfloat16),
                        pltpu.VMEM((seq_len, HEAD_DIM), jnp.bfloat16), pltpu.VMEM((HEAD_DIM, seq_len), jnp.bfloat16),
                        pltpu.VMEM((seq_len, HEAD_DIM), jnp.bfloat16), pltpu.VMEM((seq_len, HEAD_DIM), jnp.bfloat16),
                        pltpu.VMEM((seq_len, HEAD_DIM), jnp.float32), pltpu.VMEM((seq_len, HEAD_DIM), jnp.float32)],
        name="attention_backward",
        cost_estimate=pl.CostEstimate(flops=heads * 5 * 2 * seq_len * 512 * 128, bytes_accessed=inner * seq_len * 16, transcendentals=heads * seq_len * 512),
    )(mixed, mixed, mixed, cosine, sine, qaug, kaug, att, lse, d_att)


EPSILON = 1e-05
GELU_SCALE = 0.7978845608028654
GELU_CUBE = 0.044715
SEGMENTS = 9
GRIDS = {16: (4, 2, 2)}


def row_layout(lengths, pad_count, seq_len, half_dim):
    position = jnp.arange(seq_len, dtype=jnp.int32)
    doc_ends = jnp.cumsum(lengths)
    passed = position[None, :] >= doc_ends[:, None]
    segment = jnp.sum(passed.astype(jnp.int32), axis=0)
    start_at = jnp.sum(jnp.where(passed, lengths[:, None], 0), axis=0)
    pad_start = seq_len - pad_count
    is_live = position < pad_start
    segment = jnp.where(is_live, segment, lengths.shape[0])
    start_at = jnp.where(is_live, start_at, pad_start)
    offset = (position - start_at).astype(jnp.float32)
    frequencies = jnp.exp(-math.log(10000.0) * jnp.arange(half_dim, dtype=jnp.float32) / half_dim)
    angles = frequencies[:, None] * offset[None, :]
    kind = jnp.arange(AUG, dtype=jnp.int32)[:, None]
    same = kind == segment[None, :]
    query_mark = same.astype(jnp.bfloat16)
    key_mark = jnp.where(same | (kind >= SEGMENTS), 0.0, NEGATIVE).astype(jnp.bfloat16)
    return (jnp.cos(angles), jnp.sin(angles), query_mark, key_mark)


def contract(left_side, right_side, left_dim, right_dim):
    return lax.dot_general(
        left_side, right_side, (((left_dim,), (right_dim,)), ((), ())), preferred_element_type=jnp.float32
    )


def low_add(one, other):
    return (one.astype(jnp.float32) + other.astype(jnp.float32)).astype(jnp.bfloat16)


def total_of(refs):
    value = refs[0][...].astype(jnp.float32)
    for ref in refs[1:]:
        value = value + ref[...].astype(jnp.float32)
    return value


def whiten(values):
    centred = values - jnp.mean(values, axis=-1, keepdims=True)
    scale = lax.rsqrt(jnp.mean(centred * centred, axis=-1, keepdims=True) + EPSILON)
    return centred * scale, scale


def whiten_back(white, scale, gain, grad):
    weighted = grad * gain
    return (
        weighted
        - jnp.mean(weighted, axis=-1, keepdims=True)
        - white * jnp.mean(weighted * white, axis=-1, keepdims=True)
    ) * scale


def collect(ref, row, white, grad):
    gain_part = jnp.sum(grad * white, axis=0, keepdims=True)
    bias_part = jnp.sum(grad, axis=0, keepdims=True)

    @pl.when(pl.program_id(0) == 0)
    def _():
        ref[row:row + 1, :] = gain_part
        ref[row + 1:row + 2, :] = bias_part

    @pl.when(pl.program_id(0) != 0)
    def _():
        ref[row:row + 1, :] += gain_part
        ref[row + 1:row + 2, :] += bias_part


def first_kernel(gain, bias, x, normed):
    white, _ = whiten(x[...].astype(jnp.float32))
    normed[...] = (white * gain[0:1] + bias[0:1]).astype(jnp.bfloat16)


def middle_kernel(gain, bias, x, *refs):
    *parts, middle, mlp = refs
    white, _ = whiten(total_of(parts))
    rows = x[...].astype(jnp.float32) + white * gain[1:2] + bias[1:2]
    middle[...] = rows
    white, _ = whiten(rows)
    mlp[...] = (white * gain[2:3] + bias[2:3]).astype(jnp.bfloat16)


def finish_kernel(gain, bias, middle, cot, *refs):
    *parts, out, d_mlp, sums = refs
    white, scale = whiten(total_of(parts))
    out[...] = (middle[...] + white * gain[3:4] + bias[3:4]).astype(jnp.bfloat16)
    grad = cot[...].astype(jnp.float32)
    d_mlp[...] = whiten_back(white, scale, gain[3:4], grad).astype(jnp.bfloat16)
    collect(sums, 0, white, grad)


def middle_back_kernel(count, gain, bias, middle, cot, *refs):
    att_parts, parts = refs[:count], refs[count:2 * count]
    d_middle, d_att, sums = refs[2 * count:]
    grad = total_of(parts)
    white, scale = whiten(middle[...])
    collect(sums, 2, white, grad)
    grad = cot[...].astype(jnp.float32) + whiten_back(white, scale, gain[2:3], grad)
    d_middle[...] = grad
    white, scale = whiten(total_of(att_parts))
    collect(sums, 0, white, grad)
    d_att[...] = whiten_back(white, scale, gain[1:2], grad).astype(jnp.bfloat16)


def first_back_kernel(gain, bias, x, d_middle, *refs):
    *parts, out, sums = refs
    grad = total_of(parts)
    white, scale = whiten(x[...].astype(jnp.float32))
    collect(sums, 0, white, grad)
    out[...] = (d_middle[...] + whiten_back(white, scale, gain[0:1], grad)).astype(jnp.bfloat16)


def rowwise(kernel, name, gain, bias, inputs, out_types, sum_rows=0):
    rows, width = inputs[0].shape
    block = 128
    spec = pl.BlockSpec((block, width), lambda i: (i, 0))
    fixed = pl.BlockSpec(gain.shape, lambda i: (0, 0))
    out_specs = [spec] * len(out_types)
    out_shape = [jax.ShapeDtypeStruct((rows, width), t) for t in out_types]
    if sum_rows:
        out_specs.append(pl.BlockSpec((sum_rows, width), lambda i: (0, 0)))
        out_shape.append(jax.ShapeDtypeStruct((sum_rows, width), jnp.float32))
    moved = sum(a.size * a.dtype.itemsize for a in inputs) + sum(rows * width * jnp.dtype(t).itemsize for t in out_types)
    return pl.pallas_call(
        kernel,
        grid=(rows // block,),
        in_specs=[fixed, fixed] + [spec] * len(inputs),
        out_specs=out_specs,
        out_shape=out_shape,
        name=name,
        cost_estimate=pl.CostEstimate(flops=rows * width * 20, bytes_accessed=moved, transcendentals=0),
    )(gain, bias, *inputs)


class Grid:
    def __init__(self, sizes):
        count = math.prod(sizes)
        x_size, y_size = sizes[2], sizes[1]
        plane = x_size * y_size
        index = lax.axis_index("dp")
        self.x = ([(i, i ^ 1) for i in range(count)], index % x_size)
        self.y = ([(i, i ^ x_size) for i in range(count)], (index // x_size) % y_size)
        layer = lambda i: i // plane
        place = index // plane
        self.near = ([(i, i ^ plane) for i in range(count)], place % 2)
        self.far = ([(i, i ^ (2 * plane)) for i in range(count)], place // 2)

    def small(self, values):
        for pairs, _ in (self.x, self.y, self.near, self.far):
            received = yield [(values, pairs)]
            values = low_add(values, received[0])
        return values

    def colour(self, values, order):
        for pairs, bit in order:
            half = values.shape[0] // 2
            send = lax.dynamic_slice_in_dim(values, (1 - bit) * half, half, 0)
            keep = lax.dynamic_slice_in_dim(values, bit * half, half, 0)
            received = yield [(send, pairs)]
            values = low_add(keep, received[0])
        for pairs, bit in order[:0:-1]:
            received = yield [(values, pairs)]
            other = received[0]
            values = jnp.concatenate([jnp.where(bit == 0, values, other), jnp.where(bit == 0, other, values)], axis=0)
        pairs, bit = order[0]
        received = yield [(values, pairs)]
        return values, received[0], bit

    def large(self, values):
        half = values.shape[0] // 2
        first = self.colour(values[:half], (self.x, self.y, self.near, self.far))
        second = self.colour(values[half:], (self.y, self.x, self.near, self.far))
        return both(first, second)


def both(first, second):
    one, two = next(first), next(second)
    while True:
        received = yield one + two
        ends = []
        try:
            one_next = first.send(received[:len(one)])
        except StopIteration as stop:
            ends.append(stop.value)
        try:
            two_next = second.send(received[len(one):])
        except StopIteration as stop:
            ends.append(stop.value)
        if ends:
            return ends
        one, two = one_next, two_next


class Flows:
    def __init__(self):
        self.active = []
        self.results = {}

    def launch(self, name, flow, chain):
        return self.post([(name, flow, next(flow))], chain)

    def post(self, entries, chain):
        sends = [[value for value, _ in wanted] for _, _, wanted in entries]
        chain, sends = lax.optimization_barrier((chain, sends))
        for (name, flow, wanted), values in zip(entries, sends):
            flight = [lax.ppermute(value, "dp", pairs) for value, (_, pairs) in zip(values, wanted)]
            self.active.append((name, flow, flight))
        return chain

    def step(self, chain, names=None):
        chosen = [entry for entry in self.active if names is None or entry[0] in names]
        self.active = [entry for entry in self.active if names is not None and entry[0] not in names]
        chain, flights = lax.optimization_barrier((chain, [flight for _, _, flight in chosen]))
        entries = []
        for (name, flow, _), flight in zip(chosen, flights):
            try:
                entries.append((name, flow, flow.send(flight)))
            except StopIteration as stop:
                self.results[name] = stop.value
        return self.post(entries, chain) if entries else chain


def place_kernel(slot_ref, piece, *refs):
    refs[-1][0] = piece[...].astype(jnp.float32)


def place(slot, piece, base):
    rows, width = piece.shape
    blocks = 2
    operands, in_specs, aliases = [piece], [pl.BlockSpec((rows // blocks, width), lambda i, s: (i, 0))], {}
    if base is not None:
        operands.append(base)
        in_specs.append(pl.BlockSpec(memory_space=pl.ANY))
        aliases = {2: 0}
    return pl.pallas_call(
        place_kernel,
        grid_spec=pltpu.PrefetchScalarGridSpec(
            num_scalar_prefetch=1,
            grid=(blocks,),
            in_specs=in_specs,
            out_specs=pl.BlockSpec((1, rows // blocks, width), lambda i, s: (s[0], i, 0)),
        ),
        out_shape=jax.ShapeDtypeStruct((4, rows, width), jnp.float32),
        input_output_aliases=aliases,
        name="place",
        cost_estimate=pl.CostEstimate(flops=0, bytes_accessed=rows * width * 6, transcendentals=0),
    )(slot.reshape(1).astype(jnp.int32), *operands)


def assembled(ends):
    out = None
    for which in (0, 1):
        for colour, (own, other, bit) in enumerate(ends):
            slot = 2 * colour + (bit if which == 0 else 1 - bit)
            out = place(slot, own if which == 0 else other, out)
    return out.reshape((-1,) + out.shape[2:])


def make_body(sizes):
    mp_size = sizes["mp"]
    grid_sizes = GRIDS.get(sizes["dp"])

    def pair_parts(partial_sum):
        low_part = partial_sum.astype(jnp.bfloat16)
        if mp_size == 2:
            return [low_part, lax.ppermute(low_part, "mp", [(0, 1), (1, 0)])]
        return [lax.psum(low_part, "mp")]

    def plain_sum(values):
        return lax.psum(values.astype(jnp.bfloat16), "dp").astype(jnp.float32)

    def body(tokens, doc_lengths, pad_counts, gain, bias, qkv_weight, out_weight, up_weight, down_weight, cotangent):
        row_count, seq_len, width = tokens.shape
        count = row_count * seq_len
        inner = qkv_weight.shape[2]
        layouts = [row_layout(doc_lengths[r], pad_counts[r], seq_len, HEAD_DIM // 2) for r in range(row_count)]
        rows_of = [slice(r * seq_len, (r + 1) * seq_len) for r in range(row_count)]
        low, wide = jnp.bfloat16, jnp.float32
        x = tokens.reshape(count, width)
        cot = cotangent.reshape(count, width)
        qkv = jnp.transpose(qkv_weight, (1, 0, 2))

        normed = rowwise(first_kernel, "first_norm", gain, bias, [x], [low])[0]
        mixed = jnp.stack([contract(qkv[c], normed, 0, 1).astype(low) for c in range(3)])
        forward = [attention_forward(mixed[:, :, s], *layout) for s, layout in zip(rows_of, layouts)]
        att = jnp.concatenate([f[0] for f in forward], axis=1)
        att_parts = pair_parts(contract(att, out_weight, 0, 0))
        middle, mlp = rowwise(middle_kernel, "middle_norms", gain, bias, [x] + att_parts, [wide, low])
        hidden = contract(mlp, up_weight, 1, 0)
        squared = hidden * hidden
        curve = jnp.tanh(GELU_SCALE * hidden * (1.0 + GELU_CUBE * squared))
        act = (0.5 * hidden * (1.0 + curve)).astype(low)
        slope = 0.5 * (1.0 + curve) + 0.5 * GELU_SCALE * hidden * (1.0 - curve * curve) * (
            1.0 + 3.0 * GELU_CUBE * squared
        )
        slope = slope.astype(low)
        mlp_parts = pair_parts(contract(act, down_weight, 1, 0))
        out_tokens, d_mlp, last_sums = rowwise(
            finish_kernel, "finish_norm", gain, bias, [middle, cot] + mlp_parts, [low, low], 2
        )
        down_grad = contract(act, d_mlp, 0, 0).astype(low)
        down_sum = plain_sum(down_grad)
        d_mlp, _ = lax.optimization_barrier((d_mlp, down_grad))
        d_hidden = (contract(d_mlp, down_weight, 1, 1) * slope.astype(wide)).astype(low)
        up_grad = contract(mlp, d_hidden, 0, 0).astype(low)
        grid = Grid(grid_sizes) if grid_sizes else None
        flows = Flows()

        def launch(name, values, chain, kind):
            return flows.launch(name, getattr(grid, kind)(values), chain) if grid else chain

        def step(chain, names=None):
            return flows.step(chain, names) if flows.active else chain

        d_hidden = launch("up", up_grad, d_hidden, "large")
        d_mlp_parts = pair_parts(contract(d_hidden, up_weight, 1, 1))
        d_middle, d_att, middle_sums = rowwise(
            functools.partial(middle_back_kernel, len(att_parts)),
            "middle_back",
            gain,
            bias,
            [middle, cot] + att_parts + d_mlp_parts,
            [wide, low],
            4,
        )
        out_grad = contract(att, d_att, 1, 0).astype(low)
        d_attended = contract(out_weight, d_att, 1, 1).astype(low)
        d_attended = step(d_attended)
        d_attended = launch("out", out_grad, d_attended, "small")
        d_mixed = [
            attention_backward(mixed[:, :, s], *layout, f[0], f[1], d_attended[:, s])
            for s, layout, f in zip(rows_of, layouts, forward)
        ]
        d_mixed = jnp.concatenate(d_mixed, axis=2)
        d_mixed = step(d_mixed)
        qkv_grad = jnp.concatenate([contract(normed, d_mixed[c], 0, 1).astype(low) for c in range(3)], axis=0)
        d_mixed = launch("qkv", qkv_grad, d_mixed, "large")
        d_normed = sum(contract(d_mixed[c], qkv[c], 0, 1) for c in range(3))
        d_normed_parts = pair_parts(d_normed)
        d_middle = step(d_middle, ("up", "out"))
        input_grad, first_sums = rowwise(
            first_back_kernel, "first_back", gain, bias, [x, d_middle] + d_normed_parts, [low], 2
        )
        sums = jnp.concatenate([first_sums, middle_sums, last_sums], axis=0)
        if grid is None:
            qkv_sum, out_sum, up_sum, sums = plain_sum(qkv_grad), plain_sum(out_grad), plain_sum(up_grad), plain_sum(sums)
        else:
            sums = launch("sums", sums.astype(low), sums, "small")
            while flows.active:
                sums = flows.step(sums)
            qkv_sum, up_sum = assembled(flows.results["qkv"]), assembled(flows.results["up"])
            out_sum, sums = flows.results["out"].astype(wide), flows.results["sums"].astype(wide)
        qkv_sum = jnp.transpose(qkv_sum.reshape(3, width, inner), (1, 0, 2))
        return (
            out_tokens.reshape(tokens.shape),
            input_grad.reshape(tokens.shape),
            sums[0::2],
            sums[1::2],
            qkv_sum,
            out_sum,
            up_sum,
            down_sum,
        )

    return body


def solution(mesh):
    in_specs = (
        P("dp", None, None),
        P("dp", None),
        P("dp"),
        P(),
        P(),
        P(None, None, "mp"),
        P("mp", None),
        P(None, "mp"),
        P("mp", None),
        P("dp", None, None),
    )
    out_specs = (
        P("dp", None, None),
        P("dp", None, None),
        P(),
        P(),
        P(None, None, "mp"),
        P("mp", None),
        P(None, "mp"),
        P("mp", None),
    )
    return jax.shard_map(make_body(dict(mesh.shape)), mesh=mesh, in_specs=in_specs, out_specs=out_specs, check_vma=False)
```

```python
import functools
import math

import jax, jax.numpy as jnp
from jax import lax
from jax.experimental import pallas as pl
from jax.experimental.pallas import tpu as pltpu
from jax.sharding import PartitionSpec as P

HEAD_DIM = 64
DOC_MOST = 384
NEGATIVE = -1e30
BLOCK = 256
AUG = 16


def spans(seq_len):
    block = min(BLOCK, seq_len)
    return [(q, block, max(0, q - DOC_MOST)) for q in range(0, seq_len, block)]


def dot(a, b):
    return lax.dot_general(a, b, (((1,), (0,)), ((), ())), preferred_element_type=jnp.float32)


def spin(u, cosine, sine, sign):
    half = u.shape[0] // 2
    first, second = u[:half].astype(jnp.float32), u[half:].astype(jnp.float32)
    return first * cosine - sign * second * sine, second * cosine + sign * first * sine


def turned(ref, cosine, sine, scale):
    first, second = spin(ref[0], cosine, sine, 1.0)
    return jnp.concatenate([first * scale, second * scale], axis=0).astype(jnp.bfloat16)


def causal(block):
    key = lax.broadcasted_iota(jnp.int32, (block, block), 0)
    query = lax.broadcasted_iota(jnp.int32, (block, block), 1)
    return key <= query


def masked(scores, keep, block):
    last = jnp.where(keep, scores[-block:], NEGATIVE)
    if scores.shape[0] == block:
        return last
    return jnp.concatenate([scores[:-block], last], axis=0)


def setup(q_ref, k_ref, cos_ref, sin_ref, qaug_ref, kaug_ref, qt_scr, kn_scr):
    cosine, sine = cos_ref[...], sin_ref[...]
    seq_len = q_ref.shape[-1]
    pad = jnp.zeros((128 - HEAD_DIM - AUG, seq_len), jnp.bfloat16)
    q_low = turned(q_ref, cosine, sine, HEAD_DIM ** -0.5)
    k_low = turned(k_ref, cosine, sine, 1.0)
    qt_scr[...] = jnp.concatenate([q_low, qaug_ref[...], pad], axis=0)
    k_all = jnp.concatenate([k_low, kaug_ref[...], pad], axis=0)
    kn_scr[...] = k_all.T
    return q_low, k_low


def fwd_kernel(q_ref, k_ref, v_ref, cos_ref, sin_ref, qaug_ref, kaug_ref, o_ref, lse_ref, qt_scr, kn_scr):
    seq_len = q_ref.shape[-1]
    setup(q_ref, k_ref, cos_ref, sin_ref, qaug_ref, kaug_ref, qt_scr, kn_scr)
    for start, block, low in spans(seq_len):
        high = start + block
        scores = dot(kn_scr[low:high, :], qt_scr[:, start:high])
        scores = masked(scores, causal(block), block)
        top = jnp.max(scores, axis=0, keepdims=True)
        expo = jnp.exp(scores - top)
        total = jnp.sum(expo, axis=0, keepdims=True)
        out = dot(v_ref[0, :, low:high], expo.astype(jnp.bfloat16)) / total
        o_ref[:, start:high] = out.astype(jnp.bfloat16)
        lse_ref[0, :, start:high] = top + jnp.log(total)


def bwd_kernel(q_ref, k_ref, v_ref, cos_ref, sin_ref, qaug_ref, kaug_ref, o_ref, lse_ref, do_ref,
               dm_ref, qt_scr, kn_scr, qn_scr, kt_scr, vn_scr, don_scr, dk_scr, dv_scr):
    seq_len = q_ref.shape[-1]
    cosine, sine = cos_ref[...], sin_ref[...]
    q_low, k_low = setup(q_ref, k_ref, cos_ref, sin_ref, qaug_ref, kaug_ref, qt_scr, kn_scr)
    kt_scr[...] = k_low
    both = jnp.concatenate([q_low, do_ref[...]], axis=0).T
    qn_scr[...] = both[:, :HEAD_DIM]
    don_scr[...] = both[:, HEAD_DIM:]
    vn_scr[...] = v_ref[0].T
    dk_scr[...] = jnp.zeros_like(dk_scr)
    dv_scr[...] = jnp.zeros_like(dv_scr)
    inner = jnp.sum(o_ref[...].astype(jnp.float32) * do_ref[...].astype(jnp.float32), axis=0, keepdims=True)
    for start, block, low in spans(seq_len):
        high = start + block
        scores = dot(kn_scr[low:high, :], qt_scr[:, start:high])
        scores = masked(scores, causal(block), block)
        soft = jnp.exp(scores - lse_ref[0, :, start:high])
        d_soft = dot(vn_scr[low:high, :], do_ref[:, start:high])
        d_scores = (soft * (d_soft - inner[:, start:high])).astype(jnp.bfloat16)
        d_q = dot(kt_scr[:, low:high], d_scores) * HEAD_DIM ** -0.5
        first, second = spin(d_q, cosine[:, start:high], sine[:, start:high], -1.0)
        half = HEAD_DIM // 2
        dm_ref[0, :half, start:high] = first.astype(jnp.bfloat16)
        dm_ref[0, half:, start:high] = second.astype(jnp.bfloat16)
        dk_scr[low:high, :] += dot(d_scores, qn_scr[start:high, :])
        dv_scr[low:high, :] += dot(soft.astype(jnp.bfloat16), don_scr[start:high, :])
    first, second = spin(dk_scr[...].T, cosine, sine, -1.0)
    dm_ref[1] = jnp.concatenate([first, second], axis=0).astype(jnp.bfloat16)
    dm_ref[2] = dv_scr[...].T.astype(jnp.bfloat16)


def common_specs(seq_len, first=0):
    part = lambda c: pl.BlockSpec((1, HEAD_DIM, seq_len), lambda h: (c, h + first, 0))
    whole = lambda rows: pl.BlockSpec((rows, seq_len), lambda h: (0, 0))
    half = HEAD_DIM // 2
    return [part(0), part(1), part(2), whole(half), whole(half), whole(AUG), whole(AUG)]


def attention_forward(mixed, cosine, sine, qaug, kaug):
    _, inner, seq_len = mixed.shape
    heads = inner // HEAD_DIM
    head_spec = pl.BlockSpec((HEAD_DIM, seq_len), lambda h: (h, 0))
    return pl.pallas_call(
        fwd_kernel,
        grid=(heads,),
        in_specs=common_specs(seq_len),
        out_specs=[head_spec, pl.BlockSpec((1, 1, seq_len), lambda h: (h, 0, 0))],
        out_shape=[jax.ShapeDtypeStruct((inner, seq_len), jnp.bfloat16),
                   jax.ShapeDtypeStruct((heads, 1, seq_len), jnp.float32)],
        scratch_shapes=[pltpu.VMEM((128, seq_len), jnp.bfloat16), pltpu.VMEM((seq_len, 128), jnp.bfloat16)],
        name="attention_forward",
        cost_estimate=pl.CostEstimate(flops=heads * 2 * 2 * seq_len * 512 * 128, bytes_accessed=inner * seq_len * 8, transcendentals=heads * seq_len * 512),
    )(mixed, mixed, mixed, cosine, sine, qaug, kaug)


def attention_backward(mixed, cosine, sine, qaug, kaug, att, lse, d_att, first, heads, base):
    _, inner, seq_len = mixed.shape
    head_spec = pl.BlockSpec((HEAD_DIM, seq_len), lambda h: (h + first, 0))
    operands = [mixed, mixed, mixed, cosine, sine, qaug, kaug, att, lse, d_att]
    in_specs = common_specs(seq_len, first)
    in_specs += [head_spec, pl.BlockSpec((1, 1, seq_len), lambda h: (h + first, 0, 0)), head_spec]
    aliases = {}
    if base is not None:
        operands.append(base)
        in_specs.append(pl.BlockSpec(memory_space=pl.ANY))
        aliases = {10: 0}
    return pl.pallas_call(
        bwd_kernel if base is None else bwd_kernel_onto,
        grid=(heads,),
        in_specs=in_specs,
        out_specs=pl.BlockSpec((3, HEAD_DIM, seq_len), lambda h: (0, h + first, 0)),
        out_shape=jax.ShapeDtypeStruct(mixed.shape, jnp.bfloat16),
        input_output_aliases=aliases,
        scratch_shapes=[pltpu.VMEM((128, seq_len), jnp.bfloat16), pltpu.VMEM((seq_len, 128), jnp.bfloat16),
                        pltpu.VMEM((seq_len, HEAD_DIM), jnp.bfloat16), pltpu.VMEM((HEAD_DIM, seq_len), jnp.bfloat16),
                        pltpu.VMEM((seq_len, HEAD_DIM), jnp.bfloat16), pltpu.VMEM((seq_len, HEAD_DIM), jnp.bfloat16),
                        pltpu.VMEM((seq_len, HEAD_DIM), jnp.float32), pltpu.VMEM((seq_len, HEAD_DIM), jnp.float32)],
        name="attention_backward",
        cost_estimate=pl.CostEstimate(flops=heads * 5 * 2 * seq_len * 512 * 128, bytes_accessed=heads * HEAD_DIM * seq_len * 16, transcendentals=heads * seq_len * 512),
    )(*operands)


def bwd_kernel_onto(*refs):
    bwd_kernel(*refs[:10], *refs[11:])


EPSILON = 1e-05
GELU_SCALE = 0.7978845608028654
GELU_CUBE = 0.044715
SEGMENTS = 9
GRIDS = {16: (4, 2, 2)}


def row_layout(lengths, pad_count, seq_len, half_dim):
    position = jnp.arange(seq_len, dtype=jnp.int32)
    doc_ends = jnp.cumsum(lengths)
    passed = position[None, :] >= doc_ends[:, None]
    segment = jnp.sum(passed.astype(jnp.int32), axis=0)
    start_at = jnp.sum(jnp.where(passed, lengths[:, None], 0), axis=0)
    pad_start = seq_len - pad_count
    is_live = position < pad_start
    segment = jnp.where(is_live, segment, lengths.shape[0])
    start_at = jnp.where(is_live, start_at, pad_start)
    offset = (position - start_at).astype(jnp.float32)
    frequencies = jnp.exp(-math.log(10000.0) * jnp.arange(half_dim, dtype=jnp.float32) / half_dim)
    angles = frequencies[:, None] * offset[None, :]
    kind = jnp.arange(AUG, dtype=jnp.int32)[:, None]
    same = kind == segment[None, :]
    query_mark = same.astype(jnp.bfloat16)
    key_mark = jnp.where(same | (kind >= SEGMENTS), 0.0, NEGATIVE).astype(jnp.bfloat16)
    return (jnp.cos(angles), jnp.sin(angles), query_mark, key_mark)


def contract(left_side, right_side, left_dim, right_dim):
    return lax.dot_general(
        left_side, right_side, (((left_dim,), (right_dim,)), ((), ())), preferred_element_type=jnp.float32
    )


def low_add(one, other):
    return (one.astype(jnp.float32) + other.astype(jnp.float32)).astype(jnp.bfloat16)


def total_of(refs):
    value = refs[0][...].astype(jnp.float32)
    for ref in refs[1:]:
        value = value + ref[...].astype(jnp.float32)
    return value


def whiten(values):
    centred = values - jnp.mean(values, axis=-1, keepdims=True)
    scale = lax.rsqrt(jnp.mean(centred * centred, axis=-1, keepdims=True) + EPSILON)
    return centred * scale, scale


def whiten_back(white, scale, gain, grad):
    weighted = grad * gain
    return (
        weighted
        - jnp.mean(weighted, axis=-1, keepdims=True)
        - white * jnp.mean(weighted * white, axis=-1, keepdims=True)
    ) * scale


def collect(ref, row, white, grad):
    gain_part = jnp.sum(grad * white, axis=0, keepdims=True)
    bias_part = jnp.sum(grad, axis=0, keepdims=True)

    @pl.when(pl.program_id(0) == 0)
    def _():
        ref[row:row + 1, :] = gain_part
        ref[row + 1:row + 2, :] = bias_part

    @pl.when(pl.program_id(0) != 0)
    def _():
        ref[row:row + 1, :] += gain_part
        ref[row + 1:row + 2, :] += bias_part


def first_kernel(gain, bias, x, normed):
    white, _ = whiten(x[...].astype(jnp.float32))
    normed[...] = (white * gain[0:1] + bias[0:1]).astype(jnp.bfloat16)


def middle_kernel(gain, bias, x, *refs):
    *parts, middle, mlp = refs
    white, _ = whiten(total_of(parts))
    rows = x[...].astype(jnp.float32) + white * gain[1:2] + bias[1:2]
    middle[...] = rows
    white, _ = whiten(rows)
    mlp[...] = (white * gain[2:3] + bias[2:3]).astype(jnp.bfloat16)


def finish_kernel(gain, bias, middle, cot, *refs):
    *parts, out, d_mlp, sums = refs
    white, scale = whiten(total_of(parts))
    out[...] = (middle[...] + white * gain[3:4] + bias[3:4]).astype(jnp.bfloat16)
    grad = cot[...].astype(jnp.float32)
    d_mlp[...] = whiten_back(white, scale, gain[3:4], grad).astype(jnp.bfloat16)
    collect(sums, 0, white, grad)


def middle_back_kernel(count, gain, bias, middle, cot, *refs):
    att_parts, parts = refs[:count], refs[count:2 * count]
    d_middle, d_att, sums = refs[2 * count:]
    grad = total_of(parts)
    white, scale = whiten(middle[...])
    collect(sums, 2, white, grad)
    grad = cot[...].astype(jnp.float32) + whiten_back(white, scale, gain[2:3], grad)
    d_middle[...] = grad
    white, scale = whiten(total_of(att_parts))
    collect(sums, 0, white, grad)
    d_att[...] = whiten_back(white, scale, gain[1:2], grad).astype(jnp.bfloat16)


def first_back_kernel(gain, bias, x, d_middle, *refs):
    *parts, out, sums = refs
    grad = total_of(parts)
    white, scale = whiten(x[...].astype(jnp.float32))
    collect(sums, 0, white, grad)
    out[...] = (d_middle[...] + whiten_back(white, scale, gain[0:1], grad)).astype(jnp.bfloat16)


def rowwise(kernel, name, gain, bias, inputs, out_types, sum_rows=0):
    rows, width = inputs[0].shape
    block = min(256, rows)
    spec = pl.BlockSpec((block, width), lambda i: (i, 0))
    fixed = pl.BlockSpec(gain.shape, lambda i: (0, 0))
    out_specs = [spec] * len(out_types)
    out_shape = [jax.ShapeDtypeStruct((rows, width), t) for t in out_types]
    if sum_rows:
        out_specs.append(pl.BlockSpec((sum_rows, width), lambda i: (0, 0)))
        out_shape.append(jax.ShapeDtypeStruct((sum_rows, width), jnp.float32))
    moved = sum(a.size * a.dtype.itemsize for a in inputs) + sum(rows * width * jnp.dtype(t).itemsize for t in out_types)
    return pl.pallas_call(
        kernel,
        grid=(rows // block,),
        in_specs=[fixed, fixed] + [spec] * len(inputs),
        out_specs=out_specs,
        out_shape=out_shape,
        name=name,
        cost_estimate=pl.CostEstimate(flops=rows * width * 20, bytes_accessed=moved, transcendentals=0),
    )(gain, bias, *inputs)


class Grid:
    def __init__(self, sizes):
        count = math.prod(sizes)
        x_size, y_size = sizes[2], sizes[1]
        plane = x_size * y_size
        index = lax.axis_index("dp")
        self.x = ([(i, i ^ 1) for i in range(count)], index % x_size)
        self.y = ([(i, i ^ x_size) for i in range(count)], (index // x_size) % y_size)
        layer = lambda i: i // plane
        place = index // plane
        self.near = ([(i, i ^ plane) for i in range(count)], place % 2)
        self.far = ([(i, i ^ (2 * plane)) for i in range(count)], place // 2)

    def small(self, values):
        for pairs, _ in (self.x, self.y, self.near, self.far):
            received = yield [(values, pairs)]
            values = low_add(values, received[0])
        return values

    def colour(self, values, order):
        for pairs, bit in order:
            half = values.shape[0] // 2
            send = lax.dynamic_slice_in_dim(values, (1 - bit) * half, half, 0)
            keep = lax.dynamic_slice_in_dim(values, bit * half, half, 0)
            received = yield [(send, pairs)]
            values = low_add(keep, received[0])
        for pairs, bit in order[:0:-1]:
            received = yield [(values, pairs)]
            other = received[0]
            values = jnp.concatenate([jnp.where(bit == 0, values, other), jnp.where(bit == 0, other, values)], axis=0)
        pairs, bit = order[0]
        received = yield [(values, pairs)]
        return values, received[0], bit

    def large(self, values):
        half = values.shape[0] // 2
        first = self.colour(values[:half], (self.x, self.y, self.near, self.far))
        second = self.colour(values[half:], (self.y, self.x, self.near, self.far))
        return both(first, second)


def both(first, second):
    one, two = next(first), next(second)
    while True:
        received = yield one + two
        ends = []
        try:
            one_next = first.send(received[:len(one)])
        except StopIteration as stop:
            ends.append(stop.value)
        try:
            two_next = second.send(received[len(one):])
        except StopIteration as stop:
            ends.append(stop.value)
        if ends:
            return ends
        one, two = one_next, two_next


class Flows:
    def __init__(self):
        self.active = []
        self.results = {}

    def launch(self, name, flow, chain):
        return self.post([(name, flow, next(flow))], chain)

    def post(self, entries, chain):
        sends = [[value for value, _ in wanted] for _, _, wanted in entries]
        chain, sends = lax.optimization_barrier((chain, sends))
        for (name, flow, wanted), values in zip(entries, sends):
            flight = [lax.ppermute(value, "dp", pairs) for value, (_, pairs) in zip(values, wanted)]
            self.active.append((name, flow, flight))
        return chain

    def step(self, chain, names=None):
        chosen = [entry for entry in self.active if names is None or entry[0] in names]
        self.active = [entry for entry in self.active if names is not None and entry[0] not in names]
        chain, flights = lax.optimization_barrier((chain, [flight for _, _, flight in chosen]))
        entries = []
        for (name, flow, _), flight in zip(chosen, flights):
            try:
                entries.append((name, flow, flow.send(flight)))
            except StopIteration as stop:
                self.results[name] = stop.value
        return self.post(entries, chain) if entries else chain


def place_kernel(slot_ref, piece, *refs):
    refs[-1][0] = piece[...].astype(jnp.float32)


def place(slot, piece, slots, base):
    rows, width = piece.shape
    blocks = 2
    operands, in_specs, aliases = [piece], [pl.BlockSpec((rows // blocks, width), lambda i, s: (i, 0))], {}
    if base is not None:
        operands.append(base)
        in_specs.append(pl.BlockSpec(memory_space=pl.ANY))
        aliases = {2: 0}
    return pl.pallas_call(
        place_kernel,
        grid_spec=pltpu.PrefetchScalarGridSpec(
            num_scalar_prefetch=1,
            grid=(blocks,),
            in_specs=in_specs,
            out_specs=pl.BlockSpec((1, rows // blocks, width), lambda i, s: (s[0], i, 0)),
        ),
        out_shape=jax.ShapeDtypeStruct((slots, rows, width), jnp.float32),
        input_output_aliases=aliases,
        name="place",
        cost_estimate=pl.CostEstimate(flops=0, bytes_accessed=rows * width * 6, transcendentals=0),
    )(slot.reshape(1).astype(jnp.int32), *operands)


def assembled(ends):
    out = None
    for which in (0, 1):
        for colour, (own, other, bit) in enumerate(ends):
            slot = 2 * colour + (bit if which == 0 else 1 - bit)
            out = place(slot, own if which == 0 else other, 4, out)
    return out.reshape((-1,) + out.shape[2:])


def assembled_last(ends):
    (own, other, bit), (own_last, other_last, bit_last) = ends
    out = place(1 - bit, other, 3, place(bit, own, 3, None))
    third = jnp.where(bit_last == 0, own_last, other_last)
    rest = jnp.where(bit_last == 0, other_last, own_last)
    return place(jnp.int32(2), third, 3, out), rest.astype(jnp.float32)


def make_body(sizes):
    mp_size = sizes["mp"]
    grid_sizes = GRIDS.get(sizes["dp"])

    def pair_parts(partial_sum):
        low_part = partial_sum.astype(jnp.bfloat16)
        if mp_size == 2:
            return [low_part, lax.ppermute(low_part, "mp", [(0, 1), (1, 0)])]
        return [lax.psum(low_part, "mp")]

    def plain_sum(values):
        return lax.psum(values.astype(jnp.bfloat16), "dp").astype(jnp.float32)

    def body(tokens, doc_lengths, pad_counts, gain, bias, qkv_weight, out_weight, up_weight, down_weight, cotangent):
        row_count, seq_len, width = tokens.shape
        count = row_count * seq_len
        inner = qkv_weight.shape[2]
        layouts = [row_layout(doc_lengths[r], pad_counts[r], seq_len, HEAD_DIM // 2) for r in range(row_count)]
        rows_of = [slice(r * seq_len, (r + 1) * seq_len) for r in range(row_count)]
        low, wide = jnp.bfloat16, jnp.float32
        x = tokens.reshape(count, width)
        cot = cotangent.reshape(count, width)
        qkv = jnp.transpose(qkv_weight, (1, 0, 2))

        normed = rowwise(first_kernel, "first_norm", gain, bias, [x], [low])[0]
        mixed = jnp.stack([contract(qkv[c], normed, 0, 1).astype(low) for c in range(3)])
        forward = [attention_forward(mixed[:, :, s], *layout) for s, layout in zip(rows_of, layouts)]
        att = jnp.concatenate([f[0] for f in forward], axis=1)
        att_parts = pair_parts(contract(att, out_weight, 0, 0))
        middle, mlp = rowwise(middle_kernel, "middle_norms", gain, bias, [x] + att_parts, [wide, low])
        hidden = contract(mlp, up_weight, 1, 0)
        squared = hidden * hidden
        curve = jnp.tanh(GELU_SCALE * hidden * (1.0 + GELU_CUBE * squared))
        act = (0.5 * hidden * (1.0 + curve)).astype(low)
        slope = 0.5 * (1.0 + curve) + 0.5 * GELU_SCALE * hidden * (1.0 - curve * curve) * (
            1.0 + 3.0 * GELU_CUBE * squared
        )
        slope = slope.astype(low)
        mlp_parts = pair_parts(contract(act, down_weight, 1, 0))
        out_tokens, d_mlp, last_sums = rowwise(
            finish_kernel, "finish_norm", gain, bias, [middle, cot] + mlp_parts, [low, low], 2
        )
        grid = Grid(grid_sizes) if grid_sizes else None
        flows = Flows()

        def launch(name, values, chain, kind):
            return flows.launch(name, getattr(grid, kind)(values), chain) if grid else chain

        def step(chain, names=None):
            return flows.step(chain, names) if flows.active else chain

        down_grad = contract(act, d_mlp, 0, 0).astype(low)
        d_mlp = launch("down", down_grad, d_mlp, "large")
        d_hidden = (contract(d_mlp, down_weight, 1, 1) * slope.astype(wide)).astype(low)
        up_grad = contract(mlp, d_hidden, 0, 0).astype(low)
        d_hidden = launch("up", up_grad, d_hidden, "large")
        d_mlp_norm = step(contract(d_hidden, up_weight, 1, 1).astype(low), ("down",))
        d_mlp_parts = pair_parts(d_mlp_norm)
        d_middle, d_att, middle_sums = rowwise(
            functools.partial(middle_back_kernel, len(att_parts)),
            "middle_back",
            gain,
            bias,
            [middle, cot] + att_parts + d_mlp_parts,
            [wide, low],
            4,
        )
        d_attended = step(contract(out_weight, d_att, 1, 1).astype(low))
        heads = inner // HEAD_DIM
        early = heads // 2
        both_kinds = [(0, early), (early, heads - early)] if early else [(0, heads)]
        d_mixed = [None] * row_count
        for first, size in both_kinds:
            for r, (s, layout, f) in enumerate(zip(rows_of, layouts, forward)):
                d_mixed[r] = attention_backward(
                    mixed[:, :, s], *layout, f[0], f[1], d_attended[:, s], first, size, d_mixed[r]
                )
            d_mixed, d_attended = step((d_mixed, d_attended))
        d_mixed = jnp.concatenate(d_mixed, axis=2)
        half = width // 2
        qkv_grad = [contract(normed, d_mixed[c], 0, 1).astype(low) for c in range(3)]
        out_grad = contract(att, d_att, 1, 0).astype(low)
        if grid:
            last_grad = jnp.concatenate(qkv_grad + [out_grad[:, :half], out_grad[:, half:]], axis=0)
            d_mixed = launch("last", last_grad, d_mixed, "large")
        d_normed = sum(contract(d_mixed[c], qkv[c], 0, 1) for c in range(3)).astype(low)
        d_normed = step(d_normed, ("down", "up"))
        d_normed_parts = pair_parts(d_normed)
        input_grad, first_sums = rowwise(
            first_back_kernel, "first_back", gain, bias, [x, d_middle] + d_normed_parts, [low], 2
        )
        sums = jnp.concatenate([first_sums, middle_sums, last_sums], axis=0)
        if grid is None:
            qkv_sum, out_sum = plain_sum(jnp.concatenate(qkv_grad, axis=0)), plain_sum(out_grad)
            down_sum, up_sum, sums = plain_sum(down_grad), plain_sum(up_grad), plain_sum(sums)
        else:
            kept = [input_grad]
            kept = launch("sums", sums.astype(low), kept, "small")
            done = {}
            while flows.active:
                kept = flows.step(kept)
                for name, result in flows.results.items():
                    if name in ("down", "up") and name not in done:
                        done[name] = len(kept)
                        kept = kept + [assembled(result)]
            input_grad, down_sum, up_sum = kept[0], kept[done["down"]], kept[done["up"]]
            qkv_sum, halves = assembled_last(flows.results["last"])
            out_sum = jnp.concatenate([halves[:inner], halves[inner:]], axis=1)
            sums = flows.results["sums"].astype(wide)
        qkv_sum = jnp.transpose(qkv_sum.reshape(3, width, inner), (1, 0, 2))
        return (
            out_tokens.reshape(tokens.shape),
            input_grad.reshape(tokens.shape),
            sums[0::2],
            sums[1::2],
            qkv_sum,
            out_sum,
            up_sum,
            down_sum,
        )

    return body


def solution(mesh):
    in_specs = (
        P("dp", None, None),
        P("dp", None),
        P("dp"),
        P(),
        P(),
        P(None, None, "mp"),
        P("mp", None),
        P(None, "mp"),
        P("mp", None),
        P("dp", None, None),
    )
    out_specs = (
        P("dp", None, None),
        P("dp", None, None),
        P(),
        P(),
        P(None, None, "mp"),
        P("mp", None),
        P(None, "mp"),
        P("mp", None),
    )
    return jax.shard_map(make_body(dict(mesh.shape)), mesh=mesh, in_specs=in_specs, out_specs=out_specs, check_vma=False)
```
